768 devices in a mesh: segment: 48 (over x, z), seq: 16 (over y, core).
Axes of the slice: x: 4, y: 8, z: 12, core: 2. Of those that a mesh axis runs over, the one named last changes fastest.
Arguments:
- projected: bfloat16 [48, 1024, 6144], P('segment', 'seq'), may hold values from -128 to 128
- stream_before: bfloat16 [48, 1024, 2048], P('segment', 'seq'), may hold values from -3 to 3
- out_weight: bfloat16 [48, 2048, 2048], P('segment', 'seq'), may hold values from -0.25 to 0.25
- proj_weight: bfloat16 [48, 2048, 6144], P('segment', None, 'seq'), may hold values from -0.125 to 0.125
- norm_gain: float32 [48, 2048], P('segment'), may hold values from 0.1 to 1.9
- block_mask: int32 [4, 2, 2], replicated, may hold values from 0 to 1, as said below
- token_order: int32 [1024], replicated, may hold values from 0 to 1023, each once
Outputs:
- incoming: bfloat16 [48, 1024, 2048], P('segment', 'seq')
- next_projected: bfloat16 [48, 1024, 6144], P('segment', None, 'seq')
The draws below stay inside these ranges and needn't reach their ends.
Inputs may be any that keep to these rules, and one draw needn't show every extreme that they name: Each query block may always see the key block at its own place in the window (block_mask[w, b, b] = 1).
All inputs are finite; a program needn't handle non-finite values.
Results may differ from the reference program's by a relative error of at most 0.014.
Values may be sent and summed in bfloat16 or wider, within the bound.
A program may use at most 32 MiB of HBM per device.

```python
import jax
import jax.numpy as jnp
from jax import lax

D = 2048
HEADS = 16
DH = 128
WIN = 256
BLOCK = 128
SECTIONS = 48
TOKENS = 1024
NWIN = 4
BPW = 2
N_SEQ = 16


def draw_projected(key, part):
    drawn = jax.random.truncated_normal(key, -6.0, 6.0, (SECTIONS, TOKENS, HEADS, 3, DH), jnp.float32)
    return drawn.reshape(SECTIONS, TOKENS, 3 * HEADS * DH).astype(jnp.bfloat16)


def draw_block_mask(key, part):
    random_bits = jax.random.randint(jax.random.fold_in(key, 5), (NWIN, BPW, BPW), 0, 2)
    rows_index = jnp.arange(BPW, dtype=jnp.int32)[:, None]
    cols_index = jnp.arange(BPW, dtype=jnp.int32)[None, :]
    diagonal = (rows_index == cols_index).astype(jnp.int32)
    return jnp.maximum(random_bits, diagonal[None, :, :]).astype(jnp.int32)


def level_of(key, extent, cuts, smallest, largest):
    factor_of = 1.0
    for axis_at, parts in cuts:
        heights = jax.random.uniform(jax.random.fold_in(jax.random.fold_in(key, 6), axis_at), (parts,), jnp.float32, smallest / len(cuts), largest / len(cuts))
        factor_of = factor_of * jnp.repeat(jnp.exp(heights), extent[axis_at] // parts).reshape((-1,) + (1,) * (len(extent) - 1 - axis_at))
    return factor_of


def bell_draw(own_key, dims, spread, limit, pieces=(), kind=jnp.bfloat16):
    level = level_of(own_key, dims, pieces, -0.22, 0.18) if pieces else 1.0
    entries = jax.random.normal(own_key, dims, jnp.float32) * spread * level
    return jnp.minimum(jnp.maximum(entries, -limit), limit).astype(kind)


def setup_inputs(seed: int = 0) -> dict:
    streams_of = jax.random.split(jax.random.key(seed), 8)
    projected = draw_projected(jax.random.fold_in(streams_of[7], 71), 0)
    stream_before = bell_draw(streams_of[1], (SECTIONS, TOKENS, D), 0.5, 3.0, ((0, 48), (1, 16)))
    out_weight = bell_draw(streams_of[2], (SECTIONS, D, D), (D // 4) ** -0.5, 0.25, ((0, 48), (1, 16)))
    proj_weight = bell_draw(streams_of[3], (SECTIONS, D, 3 * D), D ** -0.5, 0.125, ((0, 48), (2, 16)))
    norm_gain = jnp.clip(1.0 + 0.18 * jax.random.normal(streams_of[4], (SECTIONS, D), jnp.float32), 0.1, 1.9)
    block_mask = draw_block_mask(jax.random.fold_in(streams_of[7], 71), 0)
    token_order = jax.random.permutation(streams_of[6], TOKENS).astype(jnp.int32)
    return dict(projected=projected, stream_before=stream_before, out_weight=out_weight, proj_weight=proj_weight, norm_gain=norm_gain, block_mask=block_mask, token_order=token_order)


def attend_section(projected, token_order, allowed):
    split = projected.reshape(TOKENS, HEADS, 3, DH)[token_order]
    windows = split.reshape(TOKENS // WIN, WIN, HEADS, 3, DH).astype(jnp.float32)
    scores = jnp.einsum('wqhd,wkhd->whqk', windows[:, :, :, 0], windows[:, :, :, 1]) * DH ** (-0.5)
    masked = jnp.where(allowed[:, None], scores, -jnp.inf)
    highest = lax.optimization_barrier(jnp.max(masked, axis=-1, keepdims=True))
    weights = jnp.exp(masked - highest)
    probs = (weights / lax.optimization_barrier(jnp.sum(weights, axis=-1, keepdims=True))).astype(jnp.bfloat16)
    attended = jnp.einsum('whqk,wkhd->wqhd', probs.astype(jnp.float32), windows[:, :, :, 2]).astype(jnp.bfloat16)
    placed = jnp.zeros((TOKENS, HEADS, DH), jnp.bfloat16).at[token_order].set(attended.reshape(TOKENS, HEADS, DH))
    return placed.reshape(TOKENS, HEADS * DH)

def section_layer(inputs, token_order, allowed):
    projected, stream_before, out_weight = inputs
    placed = attend_section(projected, token_order, allowed)
    per_group = HEADS // N_SEQ * DH
    grouped = jnp.transpose(placed.reshape(TOKENS, N_SEQ, per_group), (1, 0, 2))
    weight_groups = out_weight.reshape(N_SEQ, per_group, D)

    def add_group(branch, pair):
        term = jnp.dot(pair[0], pair[1], preferred_element_type=jnp.float32).astype(jnp.bfloat16)
        term = lax.optimization_barrier(term)
        return (branch + term.astype(jnp.float32), None)
    branch, _ = lax.scan(add_group, jnp.zeros((TOKENS, D), jnp.float32), (grouped, weight_groups))
    return (stream_before.astype(jnp.float32) + branch).astype(jnp.bfloat16)

def next_layer(inputs):
    incoming, gain, proj_weight = inputs
    values = incoming.astype(jnp.float32)
    scale = lax.rsqrt(lax.optimization_barrier(jnp.mean(values * values, axis=-1, keepdims=True)) + 1e-06)
    normed = (values * scale * gain[None, :]).astype(jnp.bfloat16)
    return jnp.dot(normed, proj_weight, preferred_element_type=jnp.float32).astype(jnp.bfloat16)

def reference(projected, stream_before, out_weight, proj_weight, norm_gain, block_mask, token_order):
    allowed = jnp.repeat(jnp.repeat(block_mask, BLOCK, axis=1), BLOCK, axis=2) > 0
    stream_after = lax.map(lambda item: section_layer(item, token_order, allowed), (projected, stream_before, out_weight))
    incoming = jnp.roll(stream_after, 1, axis=0)
    next_projected = lax.map(next_layer, (incoming, norm_gain, proj_weight))
    return (incoming, next_projected)
```

```python
import functools

import jax
import jax.numpy as jnp
from jax import lax
from jax.experimental import pallas as pl
from jax.experimental.pallas import tpu as pltpu
from jax.sharding import PartitionSpec as P

DH = 128
WIN = 256
BLOCK = 128
LANES = 128
SUBS = 4
COLS = 512
HIDDEN = -1e30
BF = jnp.bfloat16
F32 = jnp.float32


def remote(src, dst, send_sem, recv_sem, device):
    return pltpu.make_async_remote_copy(
        src_ref=src,
        dst_ref=dst,
        send_sem=send_sem,
        recv_sem=recv_sem,
        device_id=device,
        device_id_type=pl.DeviceIdType.MESH,
    )


def kernel(
    n_seg, n_seq,
    order_ref, mask_ref, gain_ref, projected, stream_before, out_weight, proj_weight,
    incoming_ref, next_ref,
    qkv, perm, unperm, bias, att, placed, gathered, weight, stream, wide, total,
    rs_out, rs_in, mine, theirs,
    own_sem, pw_sem, qkv_send, qkv_recv, w_send, w_recv, wp_send, wp_recv, st_send, st_recv,
    att_send, att_recv, rs_send, rs_recv, ag_send, ag_recv, pr_send, pr_recv,
):
    n_chips = n_seq // 2
    rows, width = stream.shape
    tokens = rows * n_seq
    part = rows // SUBS
    head_cols = 3 * DH
    seg, me = lax.axis_index("segment"), lax.axis_index("seq")
    core, chip = lax.rem(me, 2), me // 2
    turn = 1 - 2 * core
    ahead = {"seq": lax.rem(chip + turn + n_chips, n_chips) * 2 + core}
    peer = {"seq": chip * 2 + 1 - core}
    seg_next, seg_last = lax.rem(seg + 1, n_seg), lax.rem(seg + n_seg - 1, n_seg)

    barrier = pltpu.get_barrier_semaphore()
    for i in range(1, n_seq):
        pl.semaphore_signal(
            barrier, inc=1, device_id={"seq": lax.rem(me + i, n_seq)},
            device_id_type=pl.DeviceIdType.MESH,
        )
    for other in (seg_next, seg_last):
        for k in range(2):
            pl.semaphore_signal(
                barrier, inc=1, device_id={"segment": other, "seq": chip * 2 + k},
                device_id_type=pl.DeviceIdType.MESH,
            )

    def block_of(j):
        return projected.at[:, pl.ds(pl.multiple_of(j * head_cols, LANES), head_cols)]

    own = pltpu.make_async_copy(block_of(me), qkv.at[me], own_sem)
    own.start()
    wide_copy = pltpu.make_async_copy(proj_weight, wide, pw_sem)
    wide_copy.start()

    pl.semaphore_wait(barrier, n_seq + 3)

    def exchange(j):
        return remote(block_of(j), qkv.at[me], qkv_send.at[j], qkv_recv.at[me], {"seq": j})

    steps = [n_chips // 2]
    for d in range(n_chips // 2 - 1, 0, -1):
        steps += [d, n_chips - d]
    for d in steps:
        for k in range(2):
            exchange(lax.rem(chip + d, n_chips) * 2 + k).start()
    exchange(chip * 2 + 1 - core).start()
    straight = {"segment": seg_next, "seq": me}
    weight_out = remote(out_weight, weight.at[core], w_send, w_recv, straight)
    weight_out.start()
    stream_out = remote(stream_before, stream, st_send, st_recv, straight)
    stream_out.start()

    tiles = tokens // LANES
    order = order_ref[...]

    for q in range(tiles):
        spread = jnp.broadcast_to(order[q : q + 1, :], (LANES, LANES)).astype(F32)
        column = jnp.transpose(spread)
        for r in range(tiles):
            there = lax.broadcasted_iota(jnp.int32, (LANES, LANES), 1) + r * LANES
            perm[q * LANES : (q + 1) * LANES, r * LANES : (r + 1) * LANES] = jnp.where(
                column == there.astype(F32), 1.0, 0.0
            ).astype(BF)

    @pl.loop(0, n_seq)
    def _(b):
        base = lax.rem(b, n_chips) * (2 * rows) + (b // n_chips) * rows
        there = lax.broadcasted_iota(jnp.int32, (rows, LANES), 0) + base
        for q in range(tiles):
            here = jnp.broadcast_to(order[q : q + 1, :], (rows, LANES))
            unperm[b, :, q * LANES : (q + 1) * LANES] = jnp.where(
                here == there, 1.0, 0.0
            ).astype(BF)

    for w in range(tokens // WIN):
        for a in range(WIN // BLOCK):
            for b in range(WIN // BLOCK):
                seen = mask_ref[(w * (WIN // BLOCK) + a) * (WIN // BLOCK) + b]
                level = (1 - jnp.minimum(seen, 1)).astype(F32) * HIDDEN
                bias[w, a * BLOCK : (a + 1) * BLOCK, b * BLOCK : (b + 1) * BLOCK] = (
                    jnp.zeros((BLOCK, BLOCK), F32) + level
                )

    weight_out.wait_recv()
    weight_pair = remote(weight.at[core], weight.at[core], wp_send, wp_recv, peer)
    weight_pair.start()
    own.wait()

    @pl.loop(1, n_seq)
    def _(i):
        j = lax.rem(me + i, n_seq)
        remote(qkv.at[j], qkv.at[j], qkv_send.at[j], qkv_recv.at[j], {"seq": j}).wait_recv()

    for w in range(tokens // WIN):
        seen = slice(w * WIN, (w + 1) * WIN)
        picked = jnp.dot(
            perm[seen, :], qkv[...].reshape(tokens, head_cols), preferred_element_type=F32
        ).astype(BF)
        scores = lax.dot_general(
            picked[:, :DH], picked[:, DH : 2 * DH], (((1,), (1,)), ((), ())),
            preferred_element_type=F32,
        )
        scores = scores * DH ** (-0.5) + bias[w]
        highest = jnp.max(scores, axis=-1, keepdims=True)
        raised = jnp.exp(scores - highest)
        probs = (raised / jnp.sum(raised, axis=-1, keepdims=True)).astype(BF)
        att[seen, :] = jnp.dot(probs, picked[:, 2 * DH :], preferred_element_type=F32).astype(BF)

    def hand_on(t, k):
        return remote(
            placed.at[t, pl.ds(k * rows, rows)], gathered.at[core, t],
            att_send.at[t, k], att_recv.at[core, t],
            {"segment": seg_next, "seq": chip * 2 + k},
        )

    @pl.loop(0, n_chips)
    def _(t):
        up = lax.rem(chip + 2 * n_chips - 1 - t, n_chips)
        down = lax.rem(chip + 1 + t, n_chips)
        both = jnp.concatenate([unperm[up], unperm[n_chips + down]], axis=0)
        placed[t] = jnp.dot(both, att[...], preferred_element_type=F32).astype(BF)
        for k in range(2):
            hand_on(t, k).start()

    other_weight = remote(
        weight.at[1 - core], weight.at[1 - core], wp_send, wp_recv, peer
    )
    other_weight.wait_recv()

    def term(t):
        for k in range(2):
            remote(
                gathered.at[k, t], gathered.at[k, t], att_send.at[t, k], att_recv.at[k, t], peer
            ).wait_recv()
        left = jnp.concatenate([gathered[0, t], gathered[1, t]], axis=1)
        for n in range(width // COLS):
            cut = slice(n * COLS, (n + 1) * COLS)
            total[:, cut] = jnp.dot(
                left, weight[:, :, cut].reshape(2 * DH, COLS), preferred_element_type=F32
            )

    def reduce_on(t, s):
        cut = pl.ds(s * part, part)
        return remote(
            rs_out.at[t, cut], rs_in.at[t, cut], rs_send.at[t, s], rs_recv.at[t, s], ahead
        )

    term(0)
    for s in range(SUBS):
        cut = pl.ds(s * part, part)
        rs_out[0, cut, :] = total[cut, :].astype(BF)
        reduce_on(0, s).start()

    @pl.loop(1, n_chips - 1)
    def _(t):
        term(t)
        for s in range(SUBS):
            cut = pl.ds(s * part, part)
            reduce_on(t - 1, s).wait_recv()
            rs_out[t, cut, :] = (total[cut, :] + rs_in[t - 1, cut, :].astype(F32)).astype(BF)
            reduce_on(t, s).start()

    def gather_on(t, s):
        cut = pl.ds(s * part, part)
        return remote(
            mine.at[t, cut], mine.at[t + 1, cut], ag_send.at[t, s], ag_recv.at[t, s], ahead
        )

    def share(t, s):
        cut = pl.ds(s * part, part)
        return remote(
            mine.at[t, cut], theirs.at[t, cut], pr_send.at[t, s], pr_recv.at[t, s], peer
        )

    term(n_chips - 1)
    stream_out.wait_recv()
    for s in range(SUBS):
        cut = pl.ds(s * part, part)
        reduce_on(n_chips - 2, s).wait_recv()
        branch = total[cut, :] + rs_in[n_chips - 2, cut, :].astype(F32)
        after = (stream[cut, :].astype(F32) + branch).astype(BF)
        incoming_ref[cut, :] = after
        widened = after.astype(F32)
        scale = lax.rsqrt(jnp.mean(widened * widened, axis=-1, keepdims=True) + 1e-06)
        mine[0, cut, :] = (widened * scale * gain_ref[...]).astype(BF)
        gather_on(0, s).start()
        share(0, s).start()

    wide_copy.wait()

    def project(t):
        for s in range(SUBS):
            share(t, s).wait_recv()
        behind = lax.rem(chip + n_chips - turn * t, n_chips) * 2 + core
        beyond = lax.rem(chip + n_chips + turn * t, n_chips) * 2 + 1 - core
        both = jnp.concatenate([mine[t], theirs[t]], axis=0)
        out = jnp.dot(both, wide[...], preferred_element_type=F32).astype(BF)
        next_ref[pl.ds(pl.multiple_of(behind * rows, rows), rows), :] = out[:rows]
        next_ref[pl.ds(pl.multiple_of(beyond * rows, rows), rows), :] = out[rows:]

    @pl.loop(1, n_chips - 1)
    def _(t):
        for s in range(SUBS):
            gather_on(t - 1, s).wait_recv()
            gather_on(t, s).start()
            share(t, s).start()
        project(t - 1)

    for s in range(SUBS):
        gather_on(n_chips - 2, s).wait_recv()
        share(n_chips - 1, s).start()
    project(n_chips - 2)

    weight_out.wait_send()
    weight_pair.wait_send()
    stream_out.wait_send()

    @pl.loop(1, n_seq)
    def _(i):
        exchange(lax.rem(me + i, n_seq)).wait_send()

    @pl.loop(0, n_chips)
    def _(t):
        for k in range(2):
            hand_on(t, k).wait_send()

    @pl.loop(0, n_chips - 1)
    def _(t):
        for s in range(SUBS):
            reduce_on(t, s).wait_send()
            gather_on(t, s).wait_send()
            share(t, s).wait_send()

    project(n_chips - 1)
    for s in range(SUBS):
        share(n_chips - 1, s).wait_send()


def local(projected, stream_before, out_weight, proj_weight, norm_gain, block_mask, token_order):
    n_seg, n_seq = lax.axis_size("segment"), lax.axis_size("seq")
    n_chips = n_seq // 2
    _, rows, width = stream_before.shape
    tokens = rows * n_seq
    head_cols = 3 * DH
    windows = tokens // WIN
    dma = pltpu.SemaphoreType.DMA
    any_space = pl.BlockSpec(memory_space=pl.ANY)
    vmem = pl.BlockSpec(memory_space=pltpu.VMEM)
    incoming, following = pl.pallas_call(
        functools.partial(kernel, n_seg, n_seq),
        out_shape=(
            jax.ShapeDtypeStruct((rows, width), BF),
            jax.ShapeDtypeStruct((tokens, head_cols), BF),
        ),
        in_specs=[
            vmem,
            pl.BlockSpec(memory_space=pltpu.SMEM),
            vmem,
            any_space,
            any_space,
            any_space,
            any_space,
        ],
        out_specs=(vmem, vmem),
        scratch_shapes=[
            pltpu.VMEM((n_seq, rows, head_cols), BF),
            pltpu.VMEM((tokens, tokens), BF),
            pltpu.VMEM((n_seq, rows, tokens), BF),
            pltpu.VMEM((windows, WIN, WIN), F32),
            pltpu.VMEM((tokens, DH), BF),
            pltpu.VMEM((n_chips, 2 * rows, DH), BF),
            pltpu.VMEM((2, n_chips, rows, DH), BF),
            pltpu.VMEM((2, DH, width), BF),
            pltpu.VMEM((rows, width), BF),
            pltpu.VMEM((width, head_cols), BF),
            pltpu.VMEM((rows, width), F32),
            pltpu.VMEM((n_chips - 1, rows, width), BF),
            pltpu.VMEM((n_chips - 1, rows, width), BF),
            pltpu.VMEM((n_chips, rows, width), BF),
            pltpu.VMEM((n_chips, rows, width), BF),
            dma, dma, dma((n_seq,)), dma((n_seq,)), dma, dma, dma, dma, dma, dma,
            dma((n_chips, 2)), dma((2, n_chips)),
            dma((n_chips - 1, SUBS)), dma((n_chips - 1, SUBS)),
            dma((n_chips - 1, SUBS)), dma((n_chips - 1, SUBS)),
            dma((n_chips, SUBS)), dma((n_chips, SUBS)),
        ],
        compiler_params=pltpu.CompilerParams(collective_id=0, has_side_effects=True),
        name="section_boundary",
    )(
        token_order.reshape(tokens // LANES, LANES),
        block_mask.reshape(-1),
        norm_gain,
        projected[0],
        stream_before[0],
        out_weight[0],
        proj_weight[0],
    )
    return (incoming[None], following[None])


def solution(mesh):
    placed = (
        P("segment", "seq", None),
        P("segment", "seq", None),
        P("segment", "seq", None),
        P("segment", None, "seq"),
        P("segment", None),
        P(),
        P(),
    )
    return jax.shard_map(
        local,
        mesh=mesh,
        in_specs=placed,
        out_specs=(P("segment", "seq", None), P("segment", None, "seq")),
        check_vma=False,
    )
```

```python
import functools

import jax
import jax.numpy as jnp
from jax import lax
from jax.experimental import pallas as pl
from jax.experimental.pallas import tpu as pltpu
from jax.sharding import PartitionSpec as P

DH = 128
WIN = 256
BLOCK = 128
LANES = 128
SUBS = 4
COLS = 512
HIDDEN = -1e30
BF = jnp.bfloat16
F32 = jnp.float32


def remote(src, dst, send_sem, recv_sem, device):
    return pltpu.make_async_remote_copy(
        src_ref=src,
        dst_ref=dst,
        send_sem=send_sem,
        recv_sem=recv_sem,
        device_id=device,
        device_id_type=pl.DeviceIdType.MESH,
    )


def kernel(
    n_seg, n_seq,
    order_ref, mask_ref, gain_ref, projected, stream_before, out_weight, proj_weight,
    incoming_ref, next_ref,
    qkv, perm, unperm, bias, att, placed, gathered, weight, stream, wide, total,
    rs_out, rs_in, mine, theirs, landed,
    own_sem, pw_sem, qkv_send, qkv_recv, w_send, w_recv, wp_send, wp_recv, st_send, st_recv,
    att_send, att_recv, rs_send, rs_recv, ag_send, ag_recv, pr_send, pr_recv,
):
    n_chips = n_seq // 2
    rows, width = stream.shape
    tokens = rows * n_seq
    part = rows // SUBS
    head_cols = 3 * DH
    seg, me = lax.axis_index("segment"), lax.axis_index("seq")
    core, chip = lax.rem(me, 2), me // 2
    turn = 1 - 2 * core
    half = n_chips // 2

    def toward(t):
        way = turn * (1 - 2 * lax.rem(t, 2))
        return {"seq": lax.rem(chip + n_chips + way, n_chips) * 2 + core}

    peer = {"seq": chip * 2 + 1 - core}
    seg_next, seg_last = lax.rem(seg + 1, n_seg), lax.rem(seg + n_seg - 1, n_seg)

    barrier = pltpu.get_barrier_semaphore()
    for i in range(1, n_seq):
        pl.semaphore_signal(
            barrier, inc=1, device_id={"seq": lax.rem(me + i, n_seq)},
            device_id_type=pl.DeviceIdType.MESH,
        )
    for other in (seg_next, seg_last):
        for k in range(2):
            pl.semaphore_signal(
                barrier, inc=1, device_id={"segment": other, "seq": chip * 2 + k},
                device_id_type=pl.DeviceIdType.MESH,
            )

    def block_of(j):
        return projected.at[:, pl.ds(pl.multiple_of(j * head_cols, LANES), head_cols)]

    own = pltpu.make_async_copy(block_of(me), qkv.at[me], own_sem)
    own.start()
    wide_copy = pltpu.make_async_copy(proj_weight, wide, pw_sem)
    wide_copy.start()

    pl.semaphore_wait(barrier, n_seq + 3)

    def exchange(j):
        return remote(block_of(j), qkv.at[me], qkv_send.at[j], qkv_recv.at[me], {"seq": j})

    steps = [half]
    for d in range(half - 1, 0, -1):
        steps += [d, n_chips - d]
    for d in steps:
        for k in range(2):
            exchange(lax.rem(chip + d, n_chips) * 2 + k).start()
    exchange(chip * 2 + 1 - core).start()
    straight = {"segment": seg_next, "seq": me}
    weight_out = remote(out_weight, weight.at[core], w_send, w_recv, straight)
    weight_out.start()
    stream_out = remote(stream_before, stream, st_send, st_recv, straight)
    stream_out.start()

    tiles = tokens // LANES
    order = order_ref[...]

    for q in range(tiles):
        spread = jnp.broadcast_to(order[q : q + 1, :], (LANES, LANES)).astype(F32)
        column = jnp.transpose(spread)
        for r in range(tiles):
            there = lax.broadcasted_iota(jnp.int32, (LANES, LANES), 1) + r * LANES
            perm[q * LANES : (q + 1) * LANES, r * LANES : (r + 1) * LANES] = jnp.where(
                column == there.astype(F32), 1.0, 0.0
            ).astype(BF)

    @pl.loop(0, n_seq)
    def _(b):
        base = lax.rem(b, n_chips) * (2 * rows) + (b // n_chips) * rows
        there = lax.broadcasted_iota(jnp.int32, (rows, LANES), 0) + base
        for q in range(tiles):
            here = jnp.broadcast_to(order[q : q + 1, :], (rows, LANES))
            unperm[b, :, q * LANES : (q + 1) * LANES] = jnp.where(
                here == there, 1.0, 0.0
            ).astype(BF)

    for a in range(WIN // BLOCK):
        for b in range(WIN // BLOCK):
            level = jnp.where(mask_ref[a, b : b + 1, :] > 0, 0.0, HIDDEN)
            for w in range(tokens // WIN):
                bias[w, a * BLOCK : (a + 1) * BLOCK, b * BLOCK : (b + 1) * BLOCK] = (
                    jnp.broadcast_to(level[:, w : w + 1], (BLOCK, BLOCK))
                )

    weight_out.wait_recv()
    weight_pair = remote(weight.at[core], weight.at[core], wp_send, wp_recv, peer)
    weight_pair.start()
    own.wait()

    @pl.loop(1, n_seq)
    def _(i):
        j = lax.rem(me + i, n_seq)
        remote(qkv.at[j], qkv.at[j], qkv_send.at[j], qkv_recv.at[j], {"seq": j}).wait_recv()

    for w in range(tokens // WIN):
        seen = slice(w * WIN, (w + 1) * WIN)
        picked = jnp.dot(
            perm[seen, :], qkv[...].reshape(tokens, head_cols), preferred_element_type=F32
        ).astype(BF)
        scores = lax.dot_general(
            picked[:, :DH], picked[:, DH : 2 * DH], (((1,), (1,)), ((), ())),
            preferred_element_type=F32,
        )
        scores = scores * DH ** (-0.5) + bias[w]
        highest = jnp.max(scores, axis=-1, keepdims=True)
        raised = jnp.exp(scores - highest)
        probs = (raised / jnp.sum(raised, axis=-1, keepdims=True)).astype(BF)
        att[seen, :] = jnp.dot(probs, picked[:, 2 * DH :], preferred_element_type=F32).astype(BF)

    def hand_on(t, k):
        return remote(
            placed.at[t, pl.ds(k * rows, rows)], gathered.at[core, t],
            att_send.at[t, k], att_recv.at[core, t],
            {"segment": seg_next, "seq": chip * 2 + k},
        )

    @pl.loop(0, n_chips)
    def _(t):
        odd = lax.rem(t, 2)
        off = (1 - 2 * odd) * (half - odd - t // 2)
        up = lax.rem(chip + n_chips + off, n_chips)
        down = lax.rem(chip + n_chips - off, n_chips)
        both = jnp.concatenate([unperm[up], unperm[n_chips + down]], axis=0)
        placed[t] = jnp.dot(both, att[...], preferred_element_type=F32).astype(BF)
        for k in range(2):
            hand_on(t, k).start()

    other_weight = remote(
        weight.at[1 - core], weight.at[1 - core], wp_send, wp_recv, peer
    )
    other_weight.wait_recv()

    def term(t, at):
        for k in range(2):
            remote(
                gathered.at[k, t], gathered.at[k, t], att_send.at[t, k], att_recv.at[k, t], peer
            ).wait_recv()
        left = jnp.concatenate([gathered[0, t], gathered[1, t]], axis=1)
        for n in range(width // COLS):
            cut = slice(n * COLS, (n + 1) * COLS)
            total[at, :, cut] = jnp.dot(
                left, weight[:, :, cut].reshape(2 * DH, COLS), preferred_element_type=F32
            )

    def reduce_on(t, s):
        cut = pl.ds(s * part, part)
        return remote(
            rs_out.at[t, cut], rs_in.at[t, cut], rs_send.at[t, s], rs_recv.at[t, s], toward(t)
        )

    def pass_on(t, at, s, first):
        cut = pl.ds(s * part, part)
        value = total[at, cut, :]
        if not first:
            reduce_on(t - 2, s).wait_recv()
            value += rs_in[t - 2, cut, :].astype(F32)
        rs_out[t, cut, :] = value.astype(BF)
        reduce_on(t, s).start()

    for t in range(2):
        term(t, t)
        for s in range(SUBS):
            pass_on(t, t, s, True)

    @pl.loop(1, half - 1)
    def _(p):
        for t in range(2):
            term(2 * p + t, t)
        for s in range(SUBS):
            for t in range(2):
                pass_on(2 * p + t, t, s, False)

    for t in range(2):
        term(n_chips - 2 + t, t)
    for s in range(SUBS):
        pass_on(n_chips - 2, 0, s, False)

    def gather_on(u, s):
        cut = pl.ds(s * part, part)
        slot = max(u - 1, 0) if isinstance(u, int) else jnp.maximum(u - 1, 0)
        return remote(
            mine.at[slot, cut], mine.at[u + 1, cut], ag_send.at[u, s], ag_recv.at[u, s], toward(u)
        )

    def share(v, s):
        cut = pl.ds(s * part, part)
        return remote(
            mine.at[v, cut], theirs.at[v, cut], pr_send.at[v, s], pr_recv.at[v, s], peer
        )

    stream_out.wait_recv()
    for s in range(SUBS):
        cut = pl.ds(s * part, part)
        branch = total[1, cut, :]
        for t in (n_chips - 3, n_chips - 2):
            reduce_on(t, s).wait_recv()
            branch += rs_in[t, cut, :].astype(F32)
        after = (stream[cut, :].astype(F32) + branch).astype(BF)
        incoming_ref[cut, :] = after
        widened = after.astype(F32)
        scale = lax.rsqrt(jnp.mean(widened * widened, axis=-1, keepdims=True) + 1e-06)
        mine[0, cut, :] = (widened * scale * gain_ref[...]).astype(BF)
        for u in range(2):
            gather_on(u, s).start()
        share(0, s).start()

    wide_copy.wait()

    def place(v, ring, out):
        way = turn * (2 * lax.rem(v, 2) - 1) * (1 - 2 * ring)
        at = lax.rem(chip + n_chips - way * ((v + 1) // 2), n_chips) * 2
        at += core if ring == 0 else 1 - core
        next_ref[pl.ds(pl.multiple_of(at * rows, rows), rows), :] = out.astype(BF)

    def piece(slots, n):
        cut = slice(n * (width // SUBS), (n + 1) * (width // SUBS))
        blocks = [buffer[v, :, cut] for v in slots for buffer in (mine, theirs)]
        out = jnp.dot(
            jnp.concatenate(blocks, axis=0), wide[cut, :], preferred_element_type=F32
        )
        span = slice(0, len(blocks) * rows)
        if n > 0:
            out += landed[span, :]
        if n < SUBS - 1:
            landed[span, :] = out
        else:
            for i, v in enumerate(slots):
                for ring in range(2):
                    at = (2 * i + ring) * rows
                    place(v, ring, out[at : at + rows])

    def arrived(slots):
        for v in slots:
            for s in range(SUBS):
                share(v, s).wait_recv()

    def round_of(a, final):
        sends = [2 * a, 2 * a + 1]
        slots = [2 * a - 1, 2 * a] if a > 0 else [0]
        for s in range(SUBS):
            for u in sends[: 1 if final else 2]:
                gather_on(u, s).wait_recv()
                if u + 2 < n_chips - 1:
                    gather_on(u + 2, s).start()
                share(u + 1, s).start()
            if s == 1:
                arrived(slots)
            if s > 0:
                piece(slots, s - 1)
        piece(slots, SUBS - 1)

    for a in range(half):
        round_of(a, a == half - 1)

    weight_out.wait_send()
    weight_pair.wait_send()
    stream_out.wait_send()

    @pl.loop(1, n_seq)
    def _(i):
        exchange(lax.rem(me + i, n_seq)).wait_send()

    @pl.loop(0, n_chips)
    def _(t):
        for k in range(2):
            hand_on(t, k).wait_send()

    @pl.loop(0, n_chips - 1)
    def _(t):
        for s in range(SUBS):
            reduce_on(t, s).wait_send()
            gather_on(t, s).wait_send()
            share(t, s).wait_send()

    last = n_chips - 1
    place(last, 0, jnp.dot(mine[last], wide[...], preferred_element_type=F32))
    arrived([last])
    place(last, 1, jnp.dot(theirs[last], wide[...], preferred_element_type=F32))
    for s in range(SUBS):
        share(last, s).wait_send()


def local(projected, stream_before, out_weight, proj_weight, norm_gain, block_mask, token_order):
    n_seg, n_seq = lax.axis_size("segment"), lax.axis_size("seq")
    n_chips = n_seq // 2
    _, rows, width = stream_before.shape
    tokens = rows * n_seq
    head_cols = 3 * DH
    windows = tokens // WIN
    dma = pltpu.SemaphoreType.DMA
    any_space = pl.BlockSpec(memory_space=pl.ANY)
    vmem = pl.BlockSpec(memory_space=pltpu.VMEM)
    incoming, following = pl.pallas_call(
        functools.partial(kernel, n_seg, n_seq),
        out_shape=(
            pltpu.VMEM((rows, width), BF),
            pltpu.VMEM((tokens, head_cols), BF),
        ),
        in_specs=[
            vmem,
            vmem,
            vmem,
            any_space,
            any_space,
            any_space,
            any_space,
        ],
        out_specs=(vmem, vmem),
        scratch_shapes=[
            pltpu.VMEM((n_seq, rows, head_cols), BF),
            pltpu.VMEM((tokens, tokens), BF),
            pltpu.VMEM((n_seq, rows, tokens), BF),
            pltpu.VMEM((windows, WIN, WIN), F32),
            pltpu.VMEM((tokens, DH), BF),
            pltpu.VMEM((n_chips, 2 * rows, DH), BF),
            pltpu.VMEM((2, n_chips, rows, DH), BF),
            pltpu.VMEM((2, DH, width), BF),
            pltpu.VMEM((rows, width), BF),
            pltpu.VMEM((width, head_cols), BF),
            pltpu.VMEM((2, rows, width), F32),
            pltpu.VMEM((n_chips - 1, rows, width), BF),
            pltpu.VMEM((n_chips - 1, rows, width), BF),
            pltpu.VMEM((n_chips, rows, width), BF),
            pltpu.VMEM((n_chips, rows, width), BF),
            pltpu.VMEM((4 * rows, head_cols), F32),
            dma, dma, dma((n_seq,)), dma((n_seq,)), dma, dma, dma, dma, dma, dma,
            dma((n_chips, 2)), dma((2, n_chips)),
            dma((n_chips - 1, SUBS)), dma((n_chips - 1, SUBS)),
            dma((n_chips - 1, SUBS)), dma((n_chips - 1, SUBS)),
            dma((n_chips, SUBS)), dma((n_chips, SUBS)),
        ],
        compiler_params=pltpu.CompilerParams(collective_id=0, has_side_effects=True),
        name="section_boundary",
    )(
        token_order.reshape(tokens // LANES, LANES),
        block_mask.transpose(1, 2, 0),
        norm_gain,
        projected[0],
        stream_before[0],
        out_weight[0],
        proj_weight[0],
    )
    return (incoming[None], following[None])


def solution(mesh):
    placed = (
        P("segment", "seq", None),
        P("segment", "seq", None),
        P("segment", "seq", None),
        P("segment", None, "seq"),
        P("segment", None),
        P(),
        P(),
    )
    return jax.shard_map(
        local,
        mesh=mesh,
        in_specs=placed,
        out_specs=(P("segment", "seq", None), P("segment", None, "seq")),
        check_vma=False,
    )
```

```python
import functools

import jax
import jax.numpy as jnp
from jax import lax
from jax.experimental import pallas as pl
from jax.experimental.pallas import tpu as pltpu
from jax.sharding import PartitionSpec as P

DH = 128
WIN = 256
BLOCK = 128
LANES = 128
SUBS = 4
COLS = 512
HIDDEN = -1e30
BF = jnp.bfloat16
F32 = jnp.float32


def remote(src, dst, send_sem, recv_sem, device):
    return pltpu.make_async_remote_copy(
        src_ref=src,
        dst_ref=dst,
        send_sem=send_sem,
        recv_sem=recv_sem,
        device_id=device,
        device_id_type=pl.DeviceIdType.MESH,
    )


def kernel(
    n_seg, n_seq,
    order_in, mask_in, gain_in, projected, stream_before, out_weight, proj_weight,
    incoming_ref, next_ref,
    order_ref, mask_ref, gain_ref, pair, value, belongs, member, seen, bias, probs, placed, gathered, weight, stream, wide, total,
    rs_out, rs_in, mine, theirs, landed,
    small_sem, own_sem, pw_sem, qkv_send, qkv_recv, w_send, w_recv, wp_send, wp_recv, st_send, st_recv,
    att_send, att_recv, rs_send, rs_recv, ag_send, ag_recv, pr_send, pr_recv,
):
    n_chips = n_seq // 2
    rows, width = stream.shape
    tokens = rows * n_seq
    part = rows // SUBS
    head_cols = 3 * DH
    seg, me = lax.axis_index("segment"), lax.axis_index("seq")
    core, chip = lax.rem(me, 2), me // 2
    turn = 1 - 2 * core
    half = n_chips // 2

    def toward(t):
        way = turn * (1 - 2 * lax.rem(t, 2))
        return {"seq": lax.rem(chip + n_chips + way, n_chips) * 2 + core}

    peer = {"seq": chip * 2 + 1 - core}
    seg_next, seg_last = lax.rem(seg + 1, n_seg), lax.rem(seg + n_seg - 1, n_seg)

    hops = [half]
    for d in range(half - 1, 0, -1):
        hops += [d, n_chips - d]

    barrier = pltpu.get_barrier_semaphore()

    def greet(device):
        pl.semaphore_signal(
            barrier, inc=1, device_id=device, device_id_type=pl.DeviceIdType.MESH
        )

    for d in hops:
        for k in range(2):
            greet({"seq": lax.rem(chip + d, n_chips) * 2 + k})
    greet(peer)
    for other in (seg_next, seg_last):
        for k in range(2):
            greet({"segment": other, "seq": chip * 2 + k})

    def block_of(j, n):
        at = j * head_cols + n * 2 * DH
        return projected.at[:, pl.ds(pl.multiple_of(at, LANES), (2 - n) * DH)]

    small = [
        pltpu.make_async_copy(there, here, small_sem.at[n])
        for n, (there, here) in enumerate(
            ((order_in, order_ref), (mask_in, mask_ref), (gain_in, gain_ref))
        )
    ]
    for copy in small:
        copy.start()
    own = [
        pltpu.make_async_copy(block_of(me, n), (pair, value)[n].at[me], own_sem.at[n])
        for n in range(2)
    ]
    for n in range(2):
        own[n].start()
    wide_copy = pltpu.make_async_copy(proj_weight, wide, pw_sem)
    wide_copy.start()

    pl.semaphore_wait(barrier, n_seq + 3)

    def exchange(j, n):
        return remote(
            block_of(j, n), (pair, value)[n].at[me], qkv_send.at[n, j], qkv_recv.at[n, me],
            {"seq": j},
        )

    def from_all(n):
        own[n].wait()

        @pl.loop(1, n_seq)
        def _(i):
            j = lax.rem(me + i, n_seq)
            there = (pair, value)[n].at[j]
            remote(there, there, qkv_send.at[n, j], qkv_recv.at[n, j], {"seq": j}).wait_recv()

    def to_all(n):
        for d in hops:
            for k in range(2):
                exchange(lax.rem(chip + d, n_chips) * 2 + k, n).start()
        exchange(chip * 2 + 1 - core, n).start()

    to_all(0)
    straight = {"segment": seg_next, "seq": me}
    weight_out = remote(out_weight, weight.at[core], w_send, w_recv, straight)
    weight_out.start()
    to_all(1)
    stream_out = remote(stream_before, stream, st_send, st_recv, straight)
    stream_out.start()

    tiles = tokens // LANES
    for copy in small:
        copy.wait()
    order = order_ref[...]

    @pl.loop(0, n_seq)
    def _(b):
        there = lax.broadcasted_iota(jnp.int32, (rows, LANES), 0) + b * rows
        for q in range(tiles):
            here = jnp.broadcast_to(order[q : q + 1, :], (rows, LANES))
            belongs[pl.ds(pl.multiple_of(b * rows, rows), rows), q * LANES : (q + 1) * LANES] = (
                jnp.where(here == there, 1.0, 0.0).astype(BF)
            )

    place_block = lax.shift_right_logical(lax.broadcasted_iota(jnp.int32, (tokens, LANES), 0), 7)
    lane = lax.broadcasted_iota(jnp.int32, (tokens, LANES), 1)
    in_block = jnp.where(place_block == lane, 1.0, 0.0).astype(BF)
    member[...] = jnp.dot(belongs[...], in_block, preferred_element_type=F32).astype(BF)

    down = lax.broadcasted_iota(jnp.int32, (LANES, LANES), 0)
    across = lax.broadcasted_iota(jnp.int32, (LANES, LANES), 1)
    sees = jnp.zeros((LANES, LANES), F32)
    per = WIN // BLOCK
    for a in range(per):
        for b in range(per):
            open_ = jnp.where(mask_ref[a, b : b + 1, :] > 0, 1.0, 0.0)
            for w in range(tokens // WIN):
                here = (down == w * per + a) & (across == w * per + b)
                level = jnp.broadcast_to(open_[:, w : w + 1], (LANES, LANES))
                sees += jnp.where(here, level, 0.0)
    seen[...] = jnp.dot(
        member[...], sees.astype(BF), preferred_element_type=F32
    ).astype(BF)

    @pl.loop(0, tiles)
    def _(r):
        cut = pl.ds(pl.multiple_of(r * LANES, LANES), LANES)
        allowed = lax.dot_general(
            seen[cut, :], member[...], (((1,), (1,)), ((), ())), preferred_element_type=F32
        )
        bias[cut, :] = (1.0 - allowed) * HIDDEN

    from_all(0)
    each = LANES // rows

    @pl.loop(0, tiles)
    def _(r):
        cut = pl.ds(pl.multiple_of(r * LANES, LANES), LANES)
        query = pair[pl.ds(r * each, each), :, :DH].reshape(LANES, DH)
        key = pair[:, :, DH:].reshape(tokens, DH)
        scores = lax.dot_general(
            query, key, (((1,), (1,)), ((), ())), preferred_element_type=F32
        )
        scores = scores * DH ** (-0.5) + bias[cut, :]
        highest = jnp.max(scores, axis=-1, keepdims=True)
        raised = jnp.exp(scores - highest)
        shares = raised * (1.0 / jnp.sum(raised, axis=-1, keepdims=True))
        probs[pl.ds(r * each, each)] = shares.astype(BF).reshape(each, rows, tokens)

    weight_out.wait_recv()
    weight_pair = remote(weight.at[core], weight.at[core], wp_send, wp_recv, peer)
    weight_pair.start()
    from_all(1)

    def hand_on(t, k):
        return remote(
            placed.at[t, pl.ds(k * rows, rows)], gathered.at[core, t],
            att_send.at[t, k], att_recv.at[core, t],
            {"segment": seg_next, "seq": chip * 2 + k},
        )

    @pl.loop(0, n_chips)
    def _(t):
        odd = lax.rem(t, 2)
        off = (1 - 2 * odd) * (half - odd - t // 2)
        up = lax.rem(chip + n_chips + off, n_chips)
        down = lax.rem(chip + n_chips - off, n_chips)
        both = jnp.concatenate([probs[up * 2], probs[down * 2 + 1]], axis=0)
        placed[t] = jnp.dot(
            both, value[...].reshape(tokens, DH), preferred_element_type=F32
        ).astype(BF)
        for k in range(2):
            hand_on(t, k).start()

    other_weight = remote(
        weight.at[1 - core], weight.at[1 - core], wp_send, wp_recv, peer
    )
    other_weight.wait_recv()

    def term(t, at):
        for k in range(2):
            remote(
                gathered.at[k, t], gathered.at[k, t], att_send.at[t, k], att_recv.at[k, t], peer
            ).wait_recv()
        left = jnp.concatenate([gathered[0, t], gathered[1, t]], axis=1)
        for n in range(width // COLS):
            cut = slice(n * COLS, (n + 1) * COLS)
            total[at, :, cut] = jnp.dot(
                left, weight[:, :, cut].reshape(2 * DH, COLS), preferred_element_type=F32
            )

    def reduce_on(t, s):
        cut = pl.ds(s * part, part)
        return remote(
            rs_out.at[t, cut], rs_in.at[t, cut], rs_send.at[t, s], rs_recv.at[t, s], toward(t)
        )

    def pass_on(t, at, s, first):
        cut = pl.ds(s * part, part)
        value = total[at, cut, :]
        if not first:
            reduce_on(t - 2, s).wait_recv()
            value += rs_in[t - 2, cut, :].astype(F32)
        rs_out[t, cut, :] = value.astype(BF)
        reduce_on(t, s).start()

    for t in range(2):
        term(t, t)
        for s in range(SUBS):
            pass_on(t, t, s, True)

    @pl.loop(1, half - 1)
    def _(p):
        for t in range(2):
            term(2 * p + t, t)
        for s in range(SUBS):
            for t in range(2):
                pass_on(2 * p + t, t, s, False)

    for t in range(2):
        term(n_chips - 2 + t, t)
    for s in range(SUBS):
        pass_on(n_chips - 2, 0, s, False)

    def gather_on(u, s):
        cut = pl.ds(s * part, part)
        slot = max(u - 1, 0) if isinstance(u, int) else jnp.maximum(u - 1, 0)
        return remote(
            mine.at[slot, cut], mine.at[u + 1, cut], ag_send.at[u, s], ag_recv.at[u, s], toward(u)
        )

    def share(v, s):
        cut = pl.ds(s * part, part)
        return remote(
            mine.at[v, cut], theirs.at[v, cut], pr_send.at[v, s], pr_recv.at[v, s], peer
        )

    stream_out.wait_recv()
    for s in range(SUBS):
        cut = pl.ds(s * part, part)
        branch = total[1, cut, :]
        for t in (n_chips - 3, n_chips - 2):
            reduce_on(t, s).wait_recv()
            branch += rs_in[t, cut, :].astype(F32)
        after = (stream[cut, :].astype(F32) + branch).astype(BF)
        incoming_ref[cut, :] = after
        widened = after.astype(F32)
        scale = lax.rsqrt(jnp.mean(widened * widened, axis=-1, keepdims=True) + 1e-06)
        mine[0, cut, :] = (widened * scale * gain_ref[...]).astype(BF)
        for u in range(2):
            gather_on(u, s).start()
        share(0, s).start()

    wide_copy.wait()

    def place(v, ring, out):
        way = turn * (2 * lax.rem(v, 2) - 1) * (1 - 2 * ring)
        at = lax.rem(chip + n_chips - way * ((v + 1) // 2), n_chips) * 2
        at += core if ring == 0 else 1 - core
        next_ref[pl.ds(pl.multiple_of(at * rows, rows), rows), :] = out.astype(BF)

    def piece(slots, n):
        cut = slice(n * (width // SUBS), (n + 1) * (width // SUBS))
        blocks = [buffer[v, :, cut] for v in slots for buffer in (mine, theirs)]
        out = jnp.dot(
            jnp.concatenate(blocks, axis=0), wide[cut, :], preferred_element_type=F32
        )
        span = slice(0, len(blocks) * rows)
        if n > 0:
            out += landed[span, :]
        if n < SUBS - 1:
            landed[span, :] = out
        else:
            for i, v in enumerate(slots):
                for ring in range(2):
                    at = (2 * i + ring) * rows
                    place(v, ring, out[at : at + rows])

    def arrived(slots):
        for v in slots:
            for s in range(SUBS):
                share(v, s).wait_recv()

    def round_of(a, final):
        sends = [2 * a, 2 * a + 1]
        slots = [2 * a - 1, 2 * a] if a > 0 else [0]
        for s in range(SUBS):
            for u in sends[: 1 if final else 2]:
                gather_on(u, s).wait_recv()
                if u + 2 < n_chips - 1:
                    gather_on(u + 2, s).start()
                share(u + 1, s).start()
            if s == 1:
                arrived(slots)
            if s > 0:
                piece(slots, s - 1)
        piece(slots, SUBS - 1)

    for a in range(half):
        round_of(a, a == half - 1)

    weight_out.wait_send()
    weight_pair.wait_send()
    stream_out.wait_send()

    @pl.loop(1, n_seq)
    def _(i):
        for n in range(2):
            exchange(lax.rem(me + i, n_seq), n).wait_send()

    @pl.loop(0, n_chips)
    def _(t):
        for k in range(2):
            hand_on(t, k).wait_send()

    @pl.loop(0, n_chips - 1)
    def _(t):
        for s in range(SUBS):
            reduce_on(t, s).wait_send()
            gather_on(t, s).wait_send()
            share(t, s).wait_send()

    last = n_chips - 1
    place(last, 0, jnp.dot(mine[last], wide[...], preferred_element_type=F32))
    arrived([last])
    place(last, 1, jnp.dot(theirs[last], wide[...], preferred_element_type=F32))
    for s in range(SUBS):
        share(last, s).wait_send()


def write_out(incoming, following, incoming_out, following_out, sem):
    copies = [
        pltpu.make_async_copy(here, there, sem.at[n])
        for n, (here, there) in enumerate(
            ((incoming, incoming_out), (following, following_out))
        )
    ]
    for copy in copies:
        copy.start()
    for copy in copies:
        copy.wait()


def local(projected, stream_before, out_weight, proj_weight, norm_gain, block_mask, token_order):
    n_seg, n_seq = lax.axis_size("segment"), lax.axis_size("seq")
    n_chips = n_seq // 2
    _, rows, width = stream_before.shape
    tokens = rows * n_seq
    head_cols = 3 * DH
    dma = pltpu.SemaphoreType.DMA
    any_space = pl.BlockSpec(memory_space=pl.ANY)
    vmem = pl.BlockSpec(memory_space=pltpu.VMEM)
    incoming, following = pl.pallas_call(
        functools.partial(kernel, n_seg, n_seq),
        out_shape=(
            pltpu.VMEM((rows, width), BF),
            pltpu.VMEM((tokens, head_cols), BF),
        ),
        in_specs=[
            any_space,
            any_space,
            any_space,
            any_space,
            any_space,
            any_space,
            any_space,
        ],
        out_specs=(vmem, vmem),
        scratch_shapes=[
            pltpu.VMEM((tokens // LANES, LANES), jnp.int32),
            pltpu.VMEM((WIN // BLOCK, WIN // BLOCK, tokens // WIN), jnp.int32),
            pltpu.VMEM((1, width), F32),
            pltpu.VMEM((n_seq, rows, 2 * DH), BF),
            pltpu.VMEM((n_seq, rows, DH), BF),
            pltpu.VMEM((tokens, tokens), BF),
            pltpu.VMEM((tokens, LANES), BF),
            pltpu.VMEM((tokens, LANES), BF),
            pltpu.VMEM((tokens, tokens), F32),
            pltpu.VMEM((n_seq, rows, tokens), BF),
            pltpu.VMEM((n_chips, 2 * rows, DH), BF),
            pltpu.VMEM((2, n_chips, rows, DH), BF),
            pltpu.VMEM((2, DH, width), BF),
            pltpu.VMEM((rows, width), BF),
            pltpu.VMEM((width, head_cols), BF),
            pltpu.VMEM((2, rows, width), F32),
            pltpu.VMEM((n_chips - 1, rows, width), BF),
            pltpu.VMEM((n_chips - 1, rows, width), BF),
            pltpu.VMEM((n_chips, rows, width), BF),
            pltpu.VMEM((n_chips, rows, width), BF),
            pltpu.VMEM((4 * rows, head_cols), F32),
            dma((3,)), dma((2,)), dma, dma((2, n_seq)), dma((2, n_seq)), dma, dma, dma, dma, dma, dma,
            dma((n_chips, 2)), dma((2, n_chips)),
            dma((n_chips - 1, SUBS)), dma((n_chips - 1, SUBS)),
            dma((n_chips - 1, SUBS)), dma((n_chips - 1, SUBS)),
            dma((n_chips, SUBS)), dma((n_chips, SUBS)),
        ],
        compiler_params=pltpu.CompilerParams(collective_id=0, has_side_effects=True),
        name="section_boundary",
    )(
        token_order.reshape(tokens // LANES, LANES),
        block_mask.transpose(1, 2, 0),
        norm_gain,
        projected[0],
        stream_before[0],
        out_weight[0],
        proj_weight[0],
    )
    incoming, following = pl.pallas_call(
        write_out,
        out_shape=(
            jax.ShapeDtypeStruct((rows, width), BF),
            jax.ShapeDtypeStruct((tokens, head_cols), BF),
        ),
        in_specs=[vmem, vmem],
        out_specs=(any_space, any_space),
        scratch_shapes=[dma((2,))],
        name="write_out",
    )(*(pltpu.with_memory_space_constraint(x, pltpu.VMEM) for x in (incoming, following)))
    return (incoming[None], following[None])


def solution(mesh):
    placed = (
        P("segment", "seq", None),
        P("segment", "seq", None),
        P("segment", "seq", None),
        P("segment", None, "seq"),
        P("segment", None),
        P(),
        P(),
    )
    return jax.shard_map(
        local,
        mesh=mesh,
        in_specs=placed,
        out_specs=(P("segment", "seq", None), P("segment", None, "seq")),
        check_vma=False,
    )
```

```python
import functools

import jax
import jax.numpy as jnp
from jax import lax
from jax.experimental import pallas as pl
from jax.experimental.pallas import tpu as pltpu
from jax.sharding import PartitionSpec as P

DH = 128
WIN = 256
BLOCK = 128
LANES = 128
SUBS = 4
LATE = 0
COLS = 512
HIDDEN = -1e30
BF = jnp.bfloat16
F32 = jnp.float32


def remote(src, dst, send_sem, recv_sem, device):
    return pltpu.make_async_remote_copy(
        src_ref=src,
        dst_ref=dst,
        send_sem=send_sem,
        recv_sem=recv_sem,
        device_id=device,
        device_id_type=pl.DeviceIdType.MESH,
    )


def kernel(
    n_seg, n_seq,
    order_in, mask_in, gain_in, projected, stream_before, out_weight, proj_weight,
    incoming_ref, next_ref,
    order_ref, mask_ref, gain_ref, pair, value, belongs, member, seen, bias, probs, placed,
    beside, gathered, near, far, stream, wide, total, rs_out, rs_in, ready, early, mine, theirs, landed,
    small_sem, own_sem, pw_sem, qkv_send, qkv_recv,
    w_sem, near_send, near_recv, far_send, far_recv, st_send, st_recv,
    by_send, by_recv, att_send, att_recv, early_send, early_recv, rs_send, rs_recv, ag_send, ag_recv, pr_send, pr_recv,
):
    n_chips = n_seq // 2
    rows, width = stream.shape
    tokens = rows * n_seq
    part = rows // SUBS
    head_cols = 3 * DH
    seg, me = lax.axis_index("segment"), lax.axis_index("seq")
    core, chip = lax.rem(me, 2), me // 2
    turn = 1 - 2 * core
    half = n_chips // 2
    mid = width // 2

    def toward(t):
        way = turn * (1 - 2 * lax.rem(t, 2))
        return {"seq": lax.rem(chip + n_chips + way, n_chips) * 2 + core}

    peer = {"seq": chip * 2 + 1 - core}
    seg_next, seg_last = lax.rem(seg + 1, n_seg), lax.rem(seg + n_seg - 1, n_seg)

    hops = [half]
    for d in range(half - 1, 0, -1):
        hops += [d, n_chips - d]

    barrier = pltpu.get_barrier_semaphore()

    def greet(device):
        pl.semaphore_signal(
            barrier, inc=1, device_id=device, device_id_type=pl.DeviceIdType.MESH
        )

    for d in hops:
        for k in range(2):
            greet({"seq": lax.rem(chip + d, n_chips) * 2 + k})
    greet(peer)
    for k in range(2):
        greet({"segment": seg_last, "seq": chip * 2 + k})

    def block_of(j, n):
        at = j * head_cols + n * 2 * DH
        return projected.at[:, pl.ds(pl.multiple_of(at, LANES), (2 - n) * DH)]

    small = [
        pltpu.make_async_copy(there, here, small_sem.at[n])
        for n, (there, here) in enumerate(
            ((order_in, order_ref), (mask_in, mask_ref), (gain_in, gain_ref))
        )
    ]
    for copy in small:
        copy.start()
    own = [
        pltpu.make_async_copy(block_of(me, n), (pair, value)[n].at[me], own_sem.at[n])
        for n in range(2)
    ]
    for n in range(2):
        own[n].start()
    wide_copy = pltpu.make_async_copy(proj_weight, wide, pw_sem)
    wide_copy.start()

    pl.semaphore_wait(barrier, n_seq + 1)

    def exchange(j, n):
        return remote(
            block_of(j, n), (pair, value)[n].at[me], qkv_send.at[n, j], qkv_recv.at[n, me],
            {"seq": j},
        )

    def from_all(n):
        own[n].wait()

        @pl.loop(1, n_seq)
        def _(i):
            j = lax.rem(me + i, n_seq)
            there = (pair, value)[n].at[j]
            remote(there, there, qkv_send.at[n, j], qkv_recv.at[n, j], {"seq": j}).wait_recv()

    def to_all(n):
        for d in hops:
            for k in range(2):
                exchange(lax.rem(chip + d, n_chips) * 2 + k, n).start()
        exchange(chip * 2 + 1 - core, n).start()

    to_all(0)
    straight = {"segment": seg_next, "seq": me}
    columns = [out_weight.at[:, pl.ds(q * mid, mid)] for q in range(2)]
    kept = pltpu.make_async_copy(columns[0], near.at[0], w_sem)
    kept.start()
    near_out = remote(columns[0], near.at[1], near_send, near_recv, peer)
    near_out.start()

    def far_out(k):
        return remote(
            columns[1], far.at[core], far_send.at[k], far_recv.at[core],
            {"segment": seg_next, "seq": chip * 2 + k},
        )

    def far_in(k):
        return remote(far.at[k], far.at[k], far_send.at[k], far_recv.at[k], peer)

    for k in range(2):
        far_out(k).start()
    to_all(1)
    stream_out = remote(stream_before, stream, st_send, st_recv, straight)
    stream_out.start()

    tiles = tokens // LANES
    for copy in small:
        copy.wait()
    order = order_ref[...]

    @pl.loop(0, n_seq)
    def _(b):
        there = lax.broadcasted_iota(jnp.int32, (rows, LANES), 0) + b * rows
        for q in range(tiles):
            here = jnp.broadcast_to(order[q : q + 1, :], (rows, LANES))
            belongs[pl.ds(pl.multiple_of(b * rows, rows), rows), q * LANES : (q + 1) * LANES] = (
                jnp.where(here == there, 1.0, 0.0).astype(BF)
            )

    place_block = lax.shift_right_logical(lax.broadcasted_iota(jnp.int32, (tokens, LANES), 0), 7)
    lane = lax.broadcasted_iota(jnp.int32, (tokens, LANES), 1)
    in_block = jnp.where(place_block == lane, 1.0, 0.0).astype(BF)
    member[...] = jnp.dot(belongs[...], in_block, preferred_element_type=F32).astype(BF)

    down = lax.broadcasted_iota(jnp.int32, (LANES, LANES), 0)
    across = lax.broadcasted_iota(jnp.int32, (LANES, LANES), 1)
    sees = jnp.zeros((LANES, LANES), F32)
    per = WIN // BLOCK
    for a in range(per):
        for b in range(per):
            open_ = jnp.where(mask_ref[a, b : b + 1, :] > 0, 1.0, 0.0)
            for w in range(tokens // WIN):
                here = (down == w * per + a) & (across == w * per + b)
                level = jnp.broadcast_to(open_[:, w : w + 1], (LANES, LANES))
                sees += jnp.where(here, level, 0.0)
    seen[...] = jnp.dot(
        member[...], sees.astype(BF), preferred_element_type=F32
    ).astype(BF)

    @pl.loop(0, tiles)
    def _(r):
        cut = pl.ds(pl.multiple_of(r * LANES, LANES), LANES)
        allowed = lax.dot_general(
            seen[cut, :], member[...], (((1,), (1,)), ((), ())), preferred_element_type=F32
        )
        bias[cut, :] = (1.0 - allowed) * HIDDEN

    from_all(0)
    each = LANES // rows

    @pl.loop(0, tiles)
    def _(r):
        cut = pl.ds(pl.multiple_of(r * LANES, LANES), LANES)
        query = pair[pl.ds(r * each, each), :, :DH].reshape(LANES, DH)
        key = pair[:, :, DH:].reshape(tokens, DH)
        scores = lax.dot_general(
            query, key, (((1,), (1,)), ((), ())), preferred_element_type=F32
        )
        scores = scores * DH ** (-0.5) + bias[cut, :]
        highest = jnp.max(scores, axis=-1, keepdims=True)
        raised = jnp.exp(scores - highest)
        shares = raised * (1.0 / jnp.sum(raised, axis=-1, keepdims=True))
        probs[pl.ds(r * each, each)] = shares.astype(BF).reshape(each, rows, tokens)

    from_all(1)

    def hand_over(t):
        other = pl.ds(pl.multiple_of((1 - core) * rows, rows), rows)
        return remote(placed.at[t, other], beside.at[t], by_send.at[t], by_recv.at[t], peer)

    def hand_on(t, k):
        return remote(
            placed.at[t, pl.ds(k * rows, rows)], gathered.at[core, t],
            att_send.at[t, k], att_recv.at[core, t],
            {"segment": seg_next, "seq": chip * 2 + k},
        )

    @pl.loop(0, n_chips)
    def _(t):
        odd = lax.rem(t, 2)
        off = (1 - 2 * odd) * (half - odd - t // 2)
        up = lax.rem(chip + n_chips + off, n_chips)
        down = lax.rem(chip + n_chips - off, n_chips)
        both = jnp.concatenate([probs[up * 2], probs[down * 2 + 1]], axis=0)
        placed[t] = jnp.dot(
            both, value[...].reshape(tokens, DH), preferred_element_type=F32
        ).astype(BF)
        hand_over(t).start()
        for k in range(2):
            hand_on(t, k).start()

    kept.wait()
    near_out.wait_recv()

    def term(q, t, at):
        if q == 0:
            hand_over(t).wait_recv()
            left = [placed[t, pl.ds(pl.multiple_of(core * rows, rows), rows), :], beside[t]]
        else:
            for k in range(2):
                remote(
                    gathered.at[k, t], gathered.at[k, t], att_send.at[t, k], att_recv.at[k, t],
                    peer,
                ).wait_recv()
            left = [gathered[0, t], gathered[1, t]]
        for n in range(mid // COLS):
            cut = slice(n * COLS, (n + 1) * COLS)
            total[q, at, :, cut] = jnp.dot(
                jnp.concatenate(left, axis=1),
                (near, far)[q][:, :, cut].reshape(2 * DH, COLS),
                preferred_element_type=F32,
            )

    def reduce_on(q, t, s):
        cut = pl.ds(s * part, part)
        return remote(
            rs_out.at[q, t, cut], rs_in.at[q, t, cut],
            rs_send.at[q, t, s], rs_recv.at[q, t, s], toward(t),
        )

    def pass_on(q, t, at, s, first):
        cut = pl.ds(s * part, part)
        running = total[q, at, cut, :]
        if not first:
            reduce_on(q, t - 2, s).wait_recv()
            running += rs_in[q, t - 2, cut, :].astype(F32)
        rs_out[q, t, cut, :] = running.astype(BF)
        reduce_on(q, t, s).start()

    def begin(q):
        for t in range(2):
            term(q, t, t)
            for s in range(SUBS):
                pass_on(q, t, t, s, True)

    def keep_on(q):
        @pl.loop(1, half - 1)
        def _(p):
            for t in range(2):
                term(q, 2 * p + t, t)
            for s in range(SUBS):
                for t in range(2):
                    pass_on(q, 2 * p + t, t, s, False)

        for t in range(2):
            term(q, n_chips - 2 + t, t)
        for s in range(SUBS):
            pass_on(q, n_chips - 2, 0, s, False)

    def branch_of(q, s):
        cut = pl.ds(s * part, part)
        branch = total[q, 1, cut, :]
        for t in (n_chips - 3, n_chips - 2):
            reduce_on(q, t, s).wait_recv()
            branch += rs_in[q, t, cut, :].astype(F32)
        return branch

    def send_early(s):
        cut = pl.ds(s * part, part)
        return remote(
            ready.at[cut], early.at[cut], early_send.at[s], early_recv.at[s], straight
        )

    begin(0)
    keep_on(0)
    if LATE:
        for s in range(SUBS):
            ready[pl.ds(s * part, part), :] = branch_of(0, s).astype(BF)
            send_early(s).start()
    for k in range(2):
        far_in(k).wait_recv()
    begin(1)
    if not LATE:
        for s in range(SUBS):
            ready[pl.ds(s * part, part), :] = branch_of(0, s).astype(BF)
            send_early(s).start()
    keep_on(1)

    def gather_on(u, s):
        cut = pl.ds(s * part, part)
        slot = max(u - 1, 0) if isinstance(u, int) else jnp.maximum(u - 1, 0)
        return remote(
            mine.at[slot, cut], mine.at[u + 1, cut], ag_send.at[u, s], ag_recv.at[u, s], toward(u)
        )

    def share(v, s):
        cut = pl.ds(s * part, part)
        return remote(
            mine.at[v, cut], theirs.at[v, cut], pr_send.at[v, s], pr_recv.at[v, s], peer
        )

    stream_out.wait_recv()
    for s in range(SUBS):
        cut = pl.ds(s * part, part)
        send_early(s).wait_recv()
        branch = jnp.concatenate([early[cut, :].astype(F32), branch_of(1, s)], axis=1)
        after = (stream[cut, :].astype(F32) + branch).astype(BF)
        incoming_ref[cut, :] = after
        widened = after.astype(F32)
        scale = lax.rsqrt(jnp.mean(widened * widened, axis=-1, keepdims=True) + 1e-06)
        mine[0, cut, :] = (widened * scale * gain_ref[...]).astype(BF)
        for u in range(2):
            gather_on(u, s).start()
        share(0, s).start()

    wide_copy.wait()

    def place(v, ring, out):
        way = turn * (2 * lax.rem(v, 2) - 1) * (1 - 2 * ring)
        at = lax.rem(chip + n_chips - way * ((v + 1) // 2), n_chips) * 2
        at += core if ring == 0 else 1 - core
        next_ref[pl.ds(pl.multiple_of(at * rows, rows), rows), :] = out.astype(BF)

    def piece(slots, n):
        cut = slice(n * (width // SUBS), (n + 1) * (width // SUBS))
        blocks = [buffer[v, :, cut] for v in slots for buffer in (mine, theirs)]
        out = jnp.dot(
            jnp.concatenate(blocks, axis=0), wide[cut, :], preferred_element_type=F32
        )
        span = slice(0, len(blocks) * rows)
        if n > 0:
            out += landed[span, :]
        if n < SUBS - 1:
            landed[span, :] = out
        else:
            for i, v in enumerate(slots):
                for ring in range(2):
                    at = (2 * i + ring) * rows
                    place(v, ring, out[at : at + rows])

    def arrived(slots):
        for v in slots:
            for s in range(SUBS):
                share(v, s).wait_recv()

    def round_of(a, final):
        sends = [2 * a, 2 * a + 1]
        slots = [2 * a - 1, 2 * a] if a > 0 else [0]
        for s in range(SUBS):
            for u in sends[: 1 if final else 2]:
                gather_on(u, s).wait_recv()
                if u + 2 < n_chips - 1:
                    gather_on(u + 2, s).start()
                share(u + 1, s).start()
            if s == 1:
                arrived(slots)
            if s > 0:
                piece(slots, s - 1)
        piece(slots, SUBS - 1)

    for a in range(half):
        round_of(a, a == half - 1)

    near_out.wait_send()
    for k in range(2):
        far_out(k).wait_send()
    for s in range(SUBS):
        send_early(s).wait_send()
    stream_out.wait_send()

    @pl.loop(1, n_seq)
    def _(i):
        for n in range(2):
            exchange(lax.rem(me + i, n_seq), n).wait_send()

    @pl.loop(0, n_chips)
    def _(t):
        for k in range(2):
            hand_on(t, k).wait_send()
        hand_over(t).wait_send()

    @pl.loop(0, n_chips - 1)
    def _(t):
        for s in range(SUBS):
            for q in range(2):
                reduce_on(q, t, s).wait_send()
            gather_on(t, s).wait_send()
            share(t, s).wait_send()

    last = n_chips - 1
    place(last, 0, jnp.dot(mine[last], wide[...], preferred_element_type=F32))
    arrived([last])
    place(last, 1, jnp.dot(theirs[last], wide[...], preferred_element_type=F32))
    for s in range(SUBS):
        share(last, s).wait_send()


def write_out(incoming, following, incoming_out, following_out, sem):
    copies = [
        pltpu.make_async_copy(here, there, sem.at[n])
        for n, (here, there) in enumerate(
            ((incoming, incoming_out), (following, following_out))
        )
    ]
    for copy in copies:
        copy.start()
    for copy in copies:
        copy.wait()


def local(projected, stream_before, out_weight, proj_weight, norm_gain, block_mask, token_order):
    n_seg, n_seq = lax.axis_size("segment"), lax.axis_size("seq")
    n_chips = n_seq // 2
    _, rows, width = stream_before.shape
    tokens = rows * n_seq
    head_cols = 3 * DH
    dma = pltpu.SemaphoreType.DMA
    any_space = pl.BlockSpec(memory_space=pl.ANY)
    vmem = pl.BlockSpec(memory_space=pltpu.VMEM)
    incoming, following = pl.pallas_call(
        functools.partial(kernel, n_seg, n_seq),
        out_shape=(
            pltpu.VMEM((rows, width), BF),
            pltpu.VMEM((tokens, head_cols), BF),
        ),
        in_specs=[
            any_space,
            any_space,
            any_space,
            any_space,
            any_space,
            any_space,
            any_space,
        ],
        out_specs=(vmem, vmem),
        scratch_shapes=[
            pltpu.VMEM((tokens // LANES, LANES), jnp.int32),
            pltpu.VMEM((WIN // BLOCK, WIN // BLOCK, tokens // WIN), jnp.int32),
            pltpu.VMEM((1, width), F32),
            pltpu.VMEM((n_seq, rows, 2 * DH), BF),
            pltpu.VMEM((n_seq, rows, DH), BF),
            pltpu.VMEM((tokens, tokens), BF),
            pltpu.VMEM((tokens, LANES), BF),
            pltpu.VMEM((tokens, LANES), BF),
            pltpu.VMEM((tokens, tokens), F32),
            pltpu.VMEM((n_seq, rows, tokens), BF),
            pltpu.VMEM((n_chips, 2 * rows, DH), BF),
            pltpu.VMEM((n_chips, rows, DH), BF),
            pltpu.VMEM((2, n_chips, rows, DH), BF),
            pltpu.VMEM((2, DH, width // 2), BF),
            pltpu.VMEM((2, DH, width // 2), BF),
            pltpu.VMEM((rows, width), BF),
            pltpu.VMEM((width, head_cols), BF),
            pltpu.VMEM((2, 2, rows, width // 2), F32),
            pltpu.VMEM((2, n_chips - 1, rows, width // 2), BF),
            pltpu.VMEM((2, n_chips - 1, rows, width // 2), BF),
            pltpu.VMEM((rows, width // 2), BF),
            pltpu.VMEM((rows, width // 2), BF),
            pltpu.VMEM((n_chips, rows, width), BF),
            pltpu.VMEM((n_chips, rows, width), BF),
            pltpu.VMEM((4 * rows, head_cols), F32),
            dma((3,)), dma((2,)), dma, dma((2, n_seq)), dma((2, n_seq)),
            dma, dma, dma, dma((2,)), dma((2,)), dma, dma,
            dma((n_chips,)), dma((n_chips,)), dma((n_chips, 2)), dma((2, n_chips)),
            dma((SUBS,)), dma((SUBS,)),
            dma((2, n_chips - 1, SUBS)), dma((2, n_chips - 1, SUBS)),
            dma((n_chips - 1, SUBS)), dma((n_chips - 1, SUBS)),
            dma((n_chips, SUBS)), dma((n_chips, SUBS)),
        ],
        compiler_params=pltpu.CompilerParams(collective_id=0, has_side_effects=True),
        name="section_boundary",
    )(
        token_order.reshape(tokens // LANES, LANES),
        block_mask.transpose(1, 2, 0),
        norm_gain,
        projected[0],
        stream_before[0],
        out_weight[0],
        proj_weight[0],
    )
    incoming, following = pl.pallas_call(
        write_out,
        out_shape=(
            jax.ShapeDtypeStruct((rows, width), BF),
            jax.ShapeDtypeStruct((tokens, head_cols), BF),
        ),
        in_specs=[vmem, vmem],
        out_specs=(any_space, any_space),
        scratch_shapes=[dma((2,))],
        name="write_out",
    )(*(pltpu.with_memory_space_constraint(x, pltpu.VMEM) for x in (incoming, following)))
    return (incoming[None], following[None])


def solution(mesh):
    placed = (
        P("segment", "seq", None),
        P("segment", "seq", None),
        P("segment", "seq", None),
        P("segment", None, "seq"),
        P("segment", None),
        P(),
        P(),
    )
    return jax.shard_map(
        local,
        mesh=mesh,
        in_specs=placed,
        out_specs=(P("segment", "seq", None), P("segment", None, "seq")),
        check_vma=False,
    )
```

```python
import functools

import jax
import jax.numpy as jnp
from jax import lax
from jax.experimental import pallas as pl
from jax.experimental.pallas import tpu as pltpu
from jax.sharding import PartitionSpec as P

DH = 128
WIN = 256
BLOCK = 128
LANES = 128
SUBS = 4
COLS = 512
HIDDEN = -1e30
BF = jnp.bfloat16
F32 = jnp.float32


def remote(src, dst, send_sem, recv_sem, device):
    return pltpu.make_async_remote_copy(
        src_ref=src,
        dst_ref=dst,
        send_sem=send_sem,
        recv_sem=recv_sem,
        device_id=device,
        device_id_type=pl.DeviceIdType.MESH,
    )


def kernel(
    n_seg, n_seq,
    order_in, mask_in, gain_in, projected, stream_before, out_weight, proj_weight,
    incoming_ref, next_ref,
    order_ref, mask_ref, gain_ref, pair, value, belongs, member, seen, bias, probs, placed,
    beside, gathered, near, far, stream, wide, total, rs_out, rs_in, ready, early, mine, theirs, landed,
    small_sem, own_sem, pw_sem, qkv_send, qkv_recv,
    w_sem, near_send, near_recv, far_send, far_recv, st_send, st_recv,
    by_send, by_recv, att_send, att_recv, early_send, early_recv, rs_send, rs_recv, ag_send, ag_recv, pr_send, pr_recv,
):
    n_chips = n_seq // 2
    rows, width = stream.shape
    tokens = rows * n_seq
    part = rows // SUBS
    head_cols = 3 * DH
    seg, me = lax.axis_index("segment"), lax.axis_index("seq")
    core, chip = lax.rem(me, 2), me // 2
    turn = 1 - 2 * core
    half = n_chips // 2
    mid = width // 2

    def toward(t):
        way = turn * (1 - 2 * lax.rem(t, 2))
        return {"seq": lax.rem(chip + n_chips + way, n_chips) * 2 + core}

    peer = {"seq": chip * 2 + 1 - core}
    seg_next, seg_last = lax.rem(seg + 1, n_seg), lax.rem(seg + n_seg - 1, n_seg)

    hops = [half]
    for d in range(half - 1, 0, -1):
        hops += [d, n_chips - d]

    barrier = pltpu.get_barrier_semaphore()

    def greet(device):
        pl.semaphore_signal(
            barrier, inc=1, device_id=device, device_id_type=pl.DeviceIdType.MESH
        )

    for d in hops:
        for k in range(2):
            greet({"seq": lax.rem(chip + d, n_chips) * 2 + k})
    greet(peer)
    for k in range(2):
        greet({"segment": seg_last, "seq": chip * 2 + k})

    def block_of(j, n):
        at = j * head_cols + n * 2 * DH
        return projected.at[:, pl.ds(pl.multiple_of(at, LANES), (2 - n) * DH)]

    small = [
        pltpu.make_async_copy(there, here, small_sem.at[n])
        for n, (there, here) in enumerate(
            ((order_in, order_ref), (mask_in, mask_ref), (gain_in, gain_ref))
        )
    ]
    for copy in small:
        copy.start()
    own = [
        pltpu.make_async_copy(block_of(me, n), (pair, value)[n].at[me], own_sem.at[n])
        for n in range(2)
    ]
    for n in range(2):
        own[n].start()
    wide_copy = pltpu.make_async_copy(proj_weight, wide, pw_sem)
    wide_copy.start()

    pl.semaphore_wait(barrier, n_seq + 1)

    def exchange(j, n):
        return remote(
            block_of(j, n), (pair, value)[n].at[me], qkv_send.at[n, j], qkv_recv.at[n, me],
            {"seq": j},
        )

    def from_all(n):
        own[n].wait()

        @pl.loop(1, n_seq)
        def _(i):
            j = lax.rem(me + i, n_seq)
            there = (pair, value)[n].at[j]
            remote(there, there, qkv_send.at[n, j], qkv_recv.at[n, j], {"seq": j}).wait_recv()

    def to_all(n):
        for d in hops:
            for k in range(2):
                exchange(lax.rem(chip + d, n_chips) * 2 + k, n).start()
        exchange(chip * 2 + 1 - core, n).start()

    to_all(0)
    straight = {"segment": seg_next, "seq": me}
    columns = [out_weight.at[:, pl.ds(q * mid, mid)] for q in range(2)]
    kept = pltpu.make_async_copy(columns[0], near.at[0], w_sem)
    kept.start()
    near_out = remote(columns[0], near.at[1], near_send, near_recv, peer)
    near_out.start()

    def far_out(k):
        return remote(
            columns[1], far.at[core], far_send.at[k], far_recv.at[core],
            {"segment": seg_next, "seq": chip * 2 + k},
        )

    def far_in(k):
        return remote(far.at[k], far.at[k], far_send.at[k], far_recv.at[k], peer)

    for k in range(2):
        far_out(k).start()
    to_all(1)
    stream_out = remote(stream_before, stream, st_send, st_recv, straight)
    stream_out.start()

    tiles = tokens // LANES
    for copy in small:
        copy.wait()
    order = order_ref[...]

    @pl.loop(0, n_seq)
    def _(b):
        there = lax.broadcasted_iota(jnp.int32, (rows, LANES), 0) + b * rows
        for q in range(tiles):
            here = jnp.broadcast_to(order[q : q + 1, :], (rows, LANES))
            belongs[pl.ds(pl.multiple_of(b * rows, rows), rows), q * LANES : (q + 1) * LANES] = (
                jnp.where(here == there, 1.0, 0.0).astype(BF)
            )

    place_block = lax.shift_right_logical(lax.broadcasted_iota(jnp.int32, (tokens, LANES), 0), 7)
    lane = lax.broadcasted_iota(jnp.int32, (tokens, LANES), 1)
    in_block = jnp.where(place_block == lane, 1.0, 0.0).astype(BF)
    member[...] = jnp.dot(belongs[...], in_block, preferred_element_type=F32).astype(BF)

    down = lax.broadcasted_iota(jnp.int32, (LANES, LANES), 0)
    across = lax.broadcasted_iota(jnp.int32, (LANES, LANES), 1)
    sees = jnp.zeros((LANES, LANES), F32)
    per = WIN // BLOCK
    for a in range(per):
        for b in range(per):
            open_ = jnp.where(mask_ref[a, b : b + 1, :] > 0, 1.0, 0.0)
            for w in range(tokens // WIN):
                here = (down == w * per + a) & (across == w * per + b)
                level = jnp.broadcast_to(open_[:, w : w + 1], (LANES, LANES))
                sees += jnp.where(here, level, 0.0)
    seen[...] = jnp.dot(
        member[...], sees.astype(BF), preferred_element_type=F32
    ).astype(BF)

    @pl.loop(0, tiles)
    def _(r):
        cut = pl.ds(pl.multiple_of(r * LANES, LANES), LANES)
        allowed = lax.dot_general(
            seen[cut, :], member[...], (((1,), (1,)), ((), ())), preferred_element_type=F32
        )
        bias[cut, :] = (1.0 - allowed) * HIDDEN

    from_all(0)
    each = LANES // rows

    @pl.loop(0, tiles)
    def _(r):
        cut = pl.ds(pl.multiple_of(r * LANES, LANES), LANES)
        query = pair[pl.ds(r * each, each), :, :DH].reshape(LANES, DH)
        key = pair[:, :, DH:].reshape(tokens, DH)
        scores = lax.dot_general(
            query, key, (((1,), (1,)), ((), ())), preferred_element_type=F32
        )
        scores = scores * DH ** (-0.5) + bias[cut, :]
        highest = jnp.max(scores, axis=-1, keepdims=True)
        raised = jnp.exp(scores - highest)
        shares = raised * (1.0 / jnp.sum(raised, axis=-1, keepdims=True))
        probs[pl.ds(r * each, each)] = shares.astype(BF).reshape(each, rows, tokens)

    from_all(1)

    def hand_over(t):
        other = pl.ds(pl.multiple_of((1 - core) * rows, rows), rows)
        return remote(placed.at[t, other], beside.at[t], by_send.at[t], by_recv.at[t], peer)

    def hand_on(t, k):
        return remote(
            placed.at[t, pl.ds(k * rows, rows)], gathered.at[core, t],
            att_send.at[t, k], att_recv.at[core, t],
            {"segment": seg_next, "seq": chip * 2 + k},
        )

    @pl.loop(0, n_chips)
    def _(t):
        odd = lax.rem(t, 2)
        off = (1 - 2 * odd) * (half - odd - t // 2)
        up = lax.rem(chip + n_chips + off, n_chips)
        down = lax.rem(chip + n_chips - off, n_chips)
        both = jnp.concatenate([probs[up * 2], probs[down * 2 + 1]], axis=0)
        placed[t] = jnp.dot(
            both, value[...].reshape(tokens, DH), preferred_element_type=F32
        ).astype(BF)
        hand_over(t).start()
        for k in range(2):
            hand_on(t, k).start()

    kept.wait()
    near_out.wait_recv()

    def term(q, t, at):
        if q == 0:
            hand_over(t).wait_recv()
            left = [placed[t, pl.ds(pl.multiple_of(core * rows, rows), rows), :], beside[t]]
        else:
            for k in range(2):
                remote(
                    gathered.at[k, t], gathered.at[k, t], att_send.at[t, k], att_recv.at[k, t],
                    peer,
                ).wait_recv()
            left = [gathered[0, t], gathered[1, t]]
        for n in range(mid // COLS):
            cut = slice(n * COLS, (n + 1) * COLS)
            total[q, at, :, cut] = jnp.dot(
                jnp.concatenate(left, axis=1),
                (near, far)[q][:, :, cut].reshape(2 * DH, COLS),
                preferred_element_type=F32,
            )

    def reduce_on(q, t, s):
        cut = pl.ds(s * part, part)
        return remote(
            rs_out.at[q, t, cut], rs_in.at[q, t, cut],
            rs_send.at[q, t, s], rs_recv.at[q, t, s], toward(t),
        )

    def pass_on(q, t, at, s, first):
        cut = pl.ds(s * part, part)
        running = total[q, at, cut, :]
        if not first:
            reduce_on(q, t - 2, s).wait_recv()
            running += rs_in[q, t - 2, cut, :].astype(F32)
        rs_out[q, t, cut, :] = running.astype(BF)
        reduce_on(q, t, s).start()

    def begin(q):
        for t in range(2):
            term(q, t, t)
            for s in range(SUBS):
                pass_on(q, t, t, s, True)

        @pl.loop(2, n_chips)
        def _(t):
            term(q, t, t)

    def keep_on(q):
        @pl.loop(1, half - 1)
        def _(p):
            for s in range(SUBS):
                for t in range(2):
                    pass_on(q, 2 * p + t, 2 * p + t, s, False)

        for s in range(SUBS):
            pass_on(q, n_chips - 2, n_chips - 2, s, False)

    def branch_of(q, s):
        cut = pl.ds(s * part, part)
        branch = total[q, n_chips - 1, cut, :]
        for t in (n_chips - 3, n_chips - 2):
            reduce_on(q, t, s).wait_recv()
            branch += rs_in[q, t, cut, :].astype(F32)
        return branch

    def send_early(s):
        cut = pl.ds(s * part, part)
        return remote(
            ready.at[cut], early.at[cut], early_send.at[s], early_recv.at[s], straight
        )

    begin(0)
    keep_on(0)
    for k in range(2):
        far_in(k).wait_recv()
    begin(1)
    for s in range(SUBS):
        ready[pl.ds(s * part, part), :] = branch_of(0, s).astype(BF)
        send_early(s).start()
    keep_on(1)

    def gather_on(u, s):
        cut = pl.ds(s * part, part)
        slot = max(u - 1, 0) if isinstance(u, int) else jnp.maximum(u - 1, 0)
        return remote(
            mine.at[slot, cut], mine.at[u + 1, cut], ag_send.at[u, s], ag_recv.at[u, s], toward(u)
        )

    def share(v, s):
        cut = pl.ds(s * part, part)
        return remote(
            mine.at[v, cut], theirs.at[v, cut], pr_send.at[v, s], pr_recv.at[v, s], peer
        )

    stream_out.wait_recv()
    for s in range(SUBS):
        cut = pl.ds(s * part, part)
        send_early(s).wait_recv()
        branch = jnp.concatenate([early[cut, :].astype(F32), branch_of(1, s)], axis=1)
        after = (stream[cut, :].astype(F32) + branch).astype(BF)
        incoming_ref[cut, :] = after
        widened = after.astype(F32)
        scale = lax.rsqrt(jnp.mean(widened * widened, axis=-1, keepdims=True) + 1e-06)
        mine[0, cut, :] = (widened * scale * gain_ref[...]).astype(BF)
        for u in range(2):
            gather_on(u, s).start()
        share(0, s).start()

    wide_copy.wait()

    def place(v, ring, out):
        way = turn * (2 * lax.rem(v, 2) - 1) * (1 - 2 * ring)
        at = lax.rem(chip + n_chips - way * ((v + 1) // 2), n_chips) * 2
        at += core if ring == 0 else 1 - core
        next_ref[pl.ds(pl.multiple_of(at * rows, rows), rows), :] = out.astype(BF)

    def piece(slots, n):
        cut = slice(n * (width // SUBS), (n + 1) * (width // SUBS))
        blocks = [buffer[v, :, cut] for v in slots for buffer in (mine, theirs)]
        out = jnp.dot(
            jnp.concatenate(blocks, axis=0), wide[cut, :], preferred_element_type=F32
        )
        span = slice(0, len(blocks) * rows)
        if n > 0:
            out += landed[span, :]
        if n < SUBS - 1:
            landed[span, :] = out
        else:
            for i, v in enumerate(slots):
                for ring in range(2):
                    at = (2 * i + ring) * rows
                    place(v, ring, out[at : at + rows])

    def arrived(slots):
        for v in slots:
            for s in range(SUBS):
                share(v, s).wait_recv()

    def round_of(a, final):
        sends = [2 * a, 2 * a + 1]
        slots = [2 * a - 1, 2 * a] if a > 0 else [0]
        for s in range(SUBS):
            for u in sends[: 1 if final else 2]:
                gather_on(u, s).wait_recv()
                if u + 2 < n_chips - 1:
                    gather_on(u + 2, s).start()
                share(u + 1, s).start()
            if s == 1:
                arrived(slots)
            if s > 0:
                piece(slots, s - 1)
        piece(slots, SUBS - 1)

    for a in range(half):
        round_of(a, a == half - 1)

    near_out.wait_send()
    for k in range(2):
        far_out(k).wait_send()
    for s in range(SUBS):
        send_early(s).wait_send()
    stream_out.wait_send()

    @pl.loop(1, n_seq)
    def _(i):
        for n in range(2):
            exchange(lax.rem(me + i, n_seq), n).wait_send()

    @pl.loop(0, n_chips)
    def _(t):
        for k in range(2):
            hand_on(t, k).wait_send()
        hand_over(t).wait_send()

    @pl.loop(0, n_chips - 1)
    def _(t):
        for s in range(SUBS):
            for q in range(2):
                reduce_on(q, t, s).wait_send()
            gather_on(t, s).wait_send()
            share(t, s).wait_send()

    last = n_chips - 1
    place(last, 0, jnp.dot(mine[last], wide[...], preferred_element_type=F32))
    arrived([last])
    place(last, 1, jnp.dot(theirs[last], wide[...], preferred_element_type=F32))
    for s in range(SUBS):
        share(last, s).wait_send()


def write_out(incoming, following, incoming_out, following_out, sem):
    copies = [
        pltpu.make_async_copy(here, there, sem.at[n])
        for n, (here, there) in enumerate(
            ((incoming, incoming_out), (following, following_out))
        )
    ]
    for copy in copies:
        copy.start()
    for copy in copies:
        copy.wait()


def local(projected, stream_before, out_weight, proj_weight, norm_gain, block_mask, token_order):
    n_seg, n_seq = lax.axis_size("segment"), lax.axis_size("seq")
    n_chips = n_seq // 2
    _, rows, width = stream_before.shape
    tokens = rows * n_seq
    head_cols = 3 * DH
    dma = pltpu.SemaphoreType.DMA
    any_space = pl.BlockSpec(memory_space=pl.ANY)
    vmem = pl.BlockSpec(memory_space=pltpu.VMEM)
    incoming, following = pl.pallas_call(
        functools.partial(kernel, n_seg, n_seq),
        out_shape=(
            pltpu.VMEM((rows, width), BF),
            pltpu.VMEM((tokens, head_cols), BF),
        ),
        in_specs=[
            any_space,
            any_space,
            any_space,
            any_space,
            any_space,
            any_space,
            any_space,
        ],
        out_specs=(vmem, vmem),
        scratch_shapes=[
            pltpu.VMEM((tokens // LANES, LANES), jnp.int32),
            pltpu.VMEM((WIN // BLOCK, WIN // BLOCK, tokens // WIN), jnp.int32),
            pltpu.VMEM((1, width), F32),
            pltpu.VMEM((n_seq, rows, 2 * DH), BF),
            pltpu.VMEM((n_seq, rows, DH), BF),
            pltpu.VMEM((tokens, tokens), BF),
            pltpu.VMEM((tokens, LANES), BF),
            pltpu.VMEM((tokens, LANES), BF),
            pltpu.VMEM((tokens, tokens), F32),
            pltpu.VMEM((n_seq, rows, tokens), BF),
            pltpu.VMEM((n_chips, 2 * rows, DH), BF),
            pltpu.VMEM((n_chips, rows, DH), BF),
            pltpu.VMEM((2, n_chips, rows, DH), BF),
            pltpu.VMEM((2, DH, width // 2), BF),
            pltpu.VMEM((2, DH, width // 2), BF),
            pltpu.VMEM((rows, width), BF),
            pltpu.VMEM((width, head_cols), BF),
            pltpu.VMEM((2, n_chips, rows, width // 2), F32),
            pltpu.VMEM((2, n_chips - 1, rows, width // 2), BF),
            pltpu.VMEM((2, n_chips - 1, rows, width // 2), BF),
            pltpu.VMEM((rows, width // 2), BF),
            pltpu.VMEM((rows, width // 2), BF),
            pltpu.VMEM((n_chips, rows, width), BF),
            pltpu.VMEM((n_chips, rows, width), BF),
            pltpu.VMEM((4 * rows, head_cols), F32),
            dma((3,)), dma((2,)), dma, dma((2, n_seq)), dma((2, n_seq)),
            dma, dma, dma, dma((2,)), dma((2,)), dma, dma,
            dma((n_chips,)), dma((n_chips,)), dma((n_chips, 2)), dma((2, n_chips)),
            dma((SUBS,)), dma((SUBS,)),
            dma((2, n_chips - 1, SUBS)), dma((2, n_chips - 1, SUBS)),
            dma((n_chips - 1, SUBS)), dma((n_chips - 1, SUBS)),
            dma((n_chips, SUBS)), dma((n_chips, SUBS)),
        ],
        compiler_params=pltpu.CompilerParams(collective_id=0, has_side_effects=True),
        name="section_boundary",
    )(
        token_order.reshape(tokens // LANES, LANES),
        block_mask.transpose(1, 2, 0),
        norm_gain,
        projected[0],
        stream_before[0],
        out_weight[0],
        proj_weight[0],
    )
    incoming, following = pl.pallas_call(
        write_out,
        out_shape=(
            jax.ShapeDtypeStruct((rows, width), BF),
            jax.ShapeDtypeStruct((tokens, head_cols), BF),
        ),
        in_specs=[vmem, vmem],
        out_specs=(any_space, any_space),
        scratch_shapes=[dma((2,))],
        name="write_out",
    )(*(pltpu.with_memory_space_constraint(x, pltpu.VMEM) for x in (incoming, following)))
    return (incoming[None], following[None])


def solution(mesh):
    placed = (
        P("segment", "seq", None),
        P("segment", "seq", None),
        P("segment", "seq", None),
        P("segment", None, "seq"),
        P("segment", None),
        P(),
        P(),
    )
    return jax.shard_map(
        local,
        mesh=mesh,
        in_specs=placed,
        out_specs=(P("segment", "seq", None), P("segment", None, "seq")),
        check_vma=False,
    )
```
